32 devices in a mesh: dp: 8 (over y, x, core), tensor: 4 (over z).
Axes of the slice: x: 2, y: 2, z: 4, core: 2. Of those that a mesh axis runs over, the one named last changes fastest.
Arguments:
- hidden_in: bfloat16 [3072, 4096], P('dp', 'tensor'), may hold values from -48 to 48
- encodings: bfloat16 [512, 128, 896], P('dp', 'tensor'), may hold values from -48 to 48
- nbr_shard: int32 [48, 2], P('dp'), may hold values from 0 to 7, all different within a row; in each aligned block of 6 rows (0 to 5, 6 to 11, ...) at most 3 rows name the same one
- nbr_row: int32 [48, 2], P('dp'), may hold values from 0 to 63
- w_query: bfloat16 [4096, 4096], P(None, 'tensor'), may hold values from -0.09375 to 0.09375
- w_key: bfloat16 [896, 4096], P(None, 'tensor'), may hold values from -0.1875 to 0.1875
- w_value: bfloat16 [896, 4096], P(None, 'tensor'), may hold values from -0.1875 to 0.1875
- w_output: bfloat16 [4096, 4096], P('tensor'), may hold values from -0.09375 to 0.09375
- cotangent: bfloat16 [3072, 4096], P('dp', 'tensor'), may hold values from -6 to 6
Outputs:
- layer_out: bfloat16 [3072, 4096], P('dp', 'tensor')
- grad_hidden: bfloat16 [3072, 4096], P('dp', 'tensor')
- grad_encodings: float32 [512, 128, 896], P('dp', 'tensor')
- grad_query: float32 [4096, 4096], P('dp', 'tensor')
- grad_key: float32 [896, 4096], P('dp', 'tensor')
- grad_value: float32 [896, 4096], P('dp', 'tensor')
- grad_output: float32 [4096, 4096], P('tensor', 'dp')
The draws below stay inside these ranges and needn't reach their ends.
Inputs may be any that keep to these rules, and one draw needn't show every extreme that they name: `nbr_shard`: in the 6 spans of one index of dp no shard is named more than 3 times, and one is named exactly 3 times in some of them; the 2 shards of a span differ.
All inputs are finite; a program needn't handle non-finite values.
Results may differ from the reference program's by a relative error of at most 0.02.
Values may be sent and summed in bfloat16 or wider, within the bound.
No kernel may reach another device: no remote copies, remote signals or barrier semaphores. Data moves between devices by JAX's collectives and lax.ppermute only.
A program may use at most 128 MiB of HBM per device.

```python
import math
import jax
import jax.numpy as jnp
import numpy as np
from jax import lax

D = 4096
HEADS = 32
HD = 128
E = 896
SPAN = 64
NB = 128
K_NBR = 2
TOK_DEV = 384
DB_DEV = 64
TOKENS = 3072
SPAN_DEV = 6
SPANS = 48
LIVE = 12
CAP = 3
DB_ROWS = 512
COLS_TP = 1024
N_DP = 8
N_TENSOR = 4


def spread_normal(key, shape):
    first = jax.random.fold_in(key, 0)
    base = jax.random.normal(first, shape, jnp.float32)
    return jnp.clip(base, -6.0, 6.0)


def draw_hidden_in(key, part):
    return spread_normal(jax.random.fold_in(key, 11), (TOKENS, D)).astype(jnp.bfloat16)


def draw_encodings(key, part):
    return spread_normal(jax.random.fold_in(key, 23), (DB_ROWS, NB, E)).astype(jnp.bfloat16)


def plant(values, own_key, least, high):
    longest = values.shape.index(max(values.shape))
    spots = []
    for shift in (0, 1):
        where = [jax.random.randint(jax.random.fold_in(own_key, axis), (), 0, length) for axis, length in enumerate(values.shape)]
        where[longest] = (where[longest] + shift) % values.shape[longest]
        spots.append(tuple(where))
    return values.at[spots[0]].set(least).at[spots[1]].set(high)


def shard_levels(stream_key, shape, cuts, least, high):
    gain = 1.0
    for dim, blocks in cuts:
        draws = jax.random.uniform(jax.random.fold_in(jax.random.fold_in(stream_key, 6), dim), (blocks,), jnp.float32, least / len(cuts), high / len(cuts))
        gain = gain * jnp.repeat(jnp.exp(draws), shape[dim] // blocks).reshape((-1,) + (1,) * (len(shape) - 1 - dim))
    return gain


def deal_out(own_key, own, number, rows, number_of, top, limit, slope):
    order = jax.random.permutation(own_key, number_of)
    packed, ordinary = shares(number_of, rows * top, limit, slope, True), shares(number_of, rows * top, limit, slope, False)
    places = jnp.arange(number_of)

    def named(sizes, rotation):
        used = int((sizes > 0).sum())
        fixed = max(1, used // 4)
        passed = fixed + (places - fixed + rotation * (used - fixed)) % max(1, number_of - fixed)
        return jnp.zeros((number_of,), jnp.int32).at[order[jnp.where(places < fixed, places, passed)]].set(jnp.asarray(sizes, jnp.int32))

    sizes = jnp.where(number % 4 == 0, named(packed, number // 4), named(ordinary, number - number // 4 - 1))
    mixed = jax.random.permutation(jax.random.fold_in(own, 3), number_of)
    giver, taker = mixed[0:number_of // 2 * 2:2], mixed[1:number_of // 2 * 2:2]
    margin = jnp.minimum(sizes[giver] - 1, limit - sizes[taker]) // 2
    margin = jnp.where((giver == order[0]) | (taker == order[0]) | (sizes[taker] == 0), 0, jnp.maximum(margin, 0))
    passed = jax.random.randint(jax.random.fold_in(own, 4), (number_of // 2,), 0, 1 << 20) % (margin + 1)
    sizes = sizes.at[giver].add(-passed).at[taker].add(passed)
    labels = jnp.searchsorted(jnp.cumsum(sizes), jnp.arange(rows * top), side="right").astype(jnp.int32)
    table = labels.reshape(top, rows).T
    table = table[jax.random.permutation(jax.random.fold_in(own, 1), rows)]
    rotation = jax.random.randint(jax.random.fold_in(own, 2), (rows, 1), 0, top)
    return jnp.take_along_axis(table, (jnp.arange(top)[None, :] + rotation) % top, axis=1)


def shares(count, total, bound, slope, full):
    weights = [(1 << 20) // math.isqrt(rank ** slope) + 1 for rank in range(1, count + 1)]
    largest = bound if full else min(bound, max(-(-total // count), total * weights[0] // sum(weights)))
    least = 1 if total - largest >= count - 1 else 0
    holding, surplus = [largest] + [least] * (count - 1), total - largest - least * (count - 1)
    while surplus > 0:
        candidates = [i for i in range(1, count) if holding[i] < largest] or [i for i in range(1, count) if holding[i] < bound]
        pool, remaining = sum([weights[i] for i in candidates]), surplus
        for i in candidates:
            addition = min(bound - holding[i], max(1, remaining * weights[i] // pool), surplus)
            holding[i] = holding[i] + addition
            surplus = surplus - addition
    return np.array(holding)


def centred(key, shape, scale, bound, shards=(), kind=jnp.bfloat16):
    entries = jax.random.normal(key, shape, jnp.float32) * scale
    if len(shards) > 0:
        entries = shard_levels(key, shape, shards, -0.22, 0.18) * entries
    return jnp.clip(entries, min=-bound, max=bound).astype(kind)


def setup_inputs(seed: int = 0) -> dict:
    key_list = jax.random.split(jax.random.key(seed), 10)
    hidden_in = draw_hidden_in(jax.random.fold_in(key_list[9], 71), 0)
    encodings = draw_encodings(jax.random.fold_in(key_list[9], 71), 0)
    nbr_shard_keys = jax.random.split(jax.random.fold_in(key_list[2], 1), SPANS // SPAN_DEV)
    nbr_shard_turns = jax.random.permutation(jax.random.fold_in(key_list[2], 3), SPANS // SPAN_DEV)
    nbr_shard = jax.vmap(lambda own, number: deal_out(jax.random.fold_in(key_list[2], 2), own, number, SPAN_DEV, N_DP, K_NBR, CAP, 2))(nbr_shard_keys, nbr_shard_turns).reshape((SPANS, K_NBR))
    nbr_row = plant(jax.random.randint(key_list[3], (SPANS, K_NBR), 0, DB_DEV), jax.random.fold_in(key_list[3], 1), 0, DB_DEV - 1).astype(jnp.int32)
    w_query = centred(key_list[4], (D, D), D ** -0.5, 0.09375, ((1, 4),))
    w_key = centred(key_list[5], (E, D), E ** -0.5, 0.1875, ((1, 4),))
    w_value = centred(key_list[6], (E, D), E ** -0.5, 0.1875, ((1, 4),))
    w_output = centred(key_list[7], (D, D), D ** -0.5, 0.09375, ((0, 4),))
    cotangent = centred(key_list[8], (TOKENS, D), 1.0, 6.0, ((0, 8), (1, 4)))
    return {"hidden_in": hidden_in, "encodings": encodings, "nbr_shard": nbr_shard, "nbr_row": nbr_row, "w_query": w_query, "w_key": w_key, "w_value": w_value, "w_output": w_output, "cotangent": cotangent}


def rounded(value):
    return lax.optimization_barrier(value.astype(jnp.bfloat16)).astype(jnp.float32)

def block_products(left, right, rows):
    left_blocks = left.reshape(-1, rows, left.shape[1])
    right_blocks = right.reshape(-1, rows, right.shape[1])

    def step(total, pair):
        part = jnp.dot(pair[0].T, pair[1], preferred_element_type=jnp.float32)
        return (total + rounded(part), None)
    start = jnp.zeros((left.shape[1], right.shape[1]), jnp.float32)
    total, unused = lax.scan(step, start, (left_blocks, right_blocks))
    return total

def reference(hidden_in, encodings, nbr_shard, nbr_row, w_query, w_key, w_value, w_output, cotangent):
    scale = 1.0 / math.sqrt(HD)
    query = jnp.dot(hidden_in, w_query, preferred_element_type=jnp.float32).astype(jnp.bfloat16)
    ids = (nbr_shard * DB_DEV + nbr_row).reshape(-1).astype(jnp.int32)
    flat_nbr = encodings[ids].reshape(-1, E)
    keys = jnp.dot(flat_nbr, w_key, preferred_element_type=jnp.float32).astype(jnp.bfloat16)
    values = jnp.dot(flat_nbr, w_value, preferred_element_type=jnp.float32).astype(jnp.bfloat16)
    qh = query.reshape(SPANS, SPAN, HEADS, HD).astype(jnp.float32)
    kh = keys.reshape(SPANS, K_NBR * NB, HEADS, HD).astype(jnp.float32)
    vh = values.reshape(SPANS, K_NBR * NB, HEADS, HD).astype(jnp.float32)
    scores = jnp.einsum('cqhd,ckhd->chqk', qh, kh) * scale
    probs = jax.nn.softmax(scores, axis=-1)
    probs_b = probs.astype(jnp.bfloat16).astype(jnp.float32)
    attended = jnp.einsum('chqk,ckhd->cqhd', probs_b, vh).astype(jnp.bfloat16).reshape(TOKENS, D)
    layer_out = jnp.dot(attended, w_output, preferred_element_type=jnp.float32).astype(jnp.bfloat16)
    grad_att = jnp.dot(cotangent, w_output.T, preferred_element_type=jnp.float32).astype(jnp.bfloat16)
    dah = grad_att.reshape(SPANS, SPAN, HEADS, HD).astype(jnp.float32)
    grad_prob = jnp.einsum('cqhd,ckhd->chqk', dah, vh)
    inner = lax.optimization_barrier(jnp.sum(grad_prob * probs, axis=-1, keepdims=True))
    grad_score = (probs * (grad_prob - inner) * scale).astype(jnp.bfloat16).astype(jnp.float32)
    grad_v = jnp.einsum('chqk,cqhd->ckhd', probs_b, dah).astype(jnp.bfloat16).reshape(-1, D)
    grad_q = jnp.einsum('chqk,ckhd->cqhd', grad_score, kh).astype(jnp.bfloat16).reshape(TOKENS, D)
    grad_k = jnp.einsum('chqk,cqhd->ckhd', grad_score, qh).astype(jnp.bfloat16).reshape(-1, D)
    grad_hidden = jnp.dot(grad_q, w_query.T, preferred_element_type=jnp.float32).astype(jnp.bfloat16)
    grad_nbr = jnp.zeros((grad_k.shape[0], E), jnp.float32)
    for part in range(N_TENSOR):
        low = part * COLS_TP
        high = low + COLS_TP
        term = jnp.dot(grad_k[:, low:high], w_key[:, low:high].T, preferred_element_type=jnp.float32)
        term = term + jnp.dot(grad_v[:, low:high], w_value[:, low:high].T, preferred_element_type=jnp.float32)
        grad_nbr = grad_nbr + rounded(term)
    grad_encodings = jnp.zeros((DB_ROWS, NB, E), jnp.float32).at[ids].add(grad_nbr.reshape(-1, NB, E))
    grad_query = block_products(hidden_in, grad_q, TOK_DEV)
    grad_key = block_products(flat_nbr, grad_k, LIVE * NB)
    grad_value = block_products(flat_nbr, grad_v, LIVE * NB)
    grad_output = block_products(attended, cotangent, TOK_DEV)
    return (layer_out, grad_hidden, grad_encodings, grad_query, grad_key, grad_value, grad_output)
```

```python
import math

import jax
import jax.numpy as jnp
from jax import lax
from jax.sharding import PartitionSpec as P

HD = 128
SPAN = 64
NB = 128
K_NBR = 2


def shards(hidden_in, encodings, nbr_shard, nbr_row, w_query, w_key, w_value, w_output, cotangent):
    n_shards = lax.axis_size("dp")
    tok_rows = hidden_in.shape[0]
    columns = w_query.shape[1]
    heads_here = columns // HD
    span_count = tok_rows // SPAN
    live_blocks = K_NBR * span_count
    capacity = max(2, 4 * span_count // n_shards)
    slot_count = n_shards * capacity
    db_blocks = encodings.shape[0]
    block_part = encodings.shape[1]
    width = encodings.shape[2]
    scale = 1.0 / math.sqrt(HD)
    owners = nbr_shard.reshape(live_blocks)
    rowids = nbr_row.reshape(live_blocks)
    order = jnp.arange(live_blocks, dtype=jnp.int32)
    earlier = (owners[:, None] == owners[None, :]) & (order[None, :] < order[:, None])
    position = jnp.sum(earlier.astype(jnp.int32), axis=1)
    slot_of = owners * capacity + position
    picked = slot_of[:, None] == jnp.arange(slot_count, dtype=jnp.int32)[None, :]
    request = jnp.sum(jnp.where(picked, rowids[:, None] + 1, 0), axis=0) - 1
    wanted = lax.all_to_all(
        request.reshape(n_shards, capacity), "dp", split_axis=0, concat_axis=0, tiled=True
    )
    table = (
        wanted.reshape(slot_count)[:, None] == jnp.arange(db_blocks, dtype=jnp.int32)[None, :]
    ).astype(jnp.bfloat16)
    outgoing = jnp.dot(
        table, encodings.reshape(db_blocks, block_part * width), preferred_element_type=jnp.float32
    )
    outgoing = outgoing.astype(jnp.bfloat16).reshape(n_shards, capacity, block_part, width)
    arrived = lax.all_to_all(outgoing, "dp", split_axis=0, concat_axis=0, tiled=True).reshape(
        slot_count, block_part, width
    )
    select = picked.astype(jnp.bfloat16)
    live = jnp.dot(
        select, arrived.reshape(slot_count, block_part * width), preferred_element_type=jnp.float32
    )
    live = live.astype(jnp.bfloat16).reshape(live_blocks, block_part, width)
    neighbours = lax.all_gather(live, "tensor", axis=1, tiled=True)
    nbr_flat = neighbours.reshape(live_blocks * NB, width)
    hidden_full = lax.all_gather(hidden_in, "tensor", axis=1, tiled=True)
    query = jnp.dot(hidden_full, w_query, preferred_element_type=jnp.float32).astype(jnp.bfloat16)
    keys = jnp.dot(nbr_flat, w_key, preferred_element_type=jnp.float32).astype(jnp.bfloat16)
    values = jnp.dot(nbr_flat, w_value, preferred_element_type=jnp.float32).astype(jnp.bfloat16)
    query_h = query.reshape(span_count, SPAN, heads_here, HD)
    keys_h = keys.reshape(span_count, K_NBR * NB, heads_here, HD)
    values_h = values.reshape(span_count, K_NBR * NB, heads_here, HD)
    scores = (
        jnp.einsum("cqhd,ckhd->chqk", query_h, keys_h, preferred_element_type=jnp.float32) * scale
    )
    probs = jax.nn.softmax(scores, axis=-1)
    probs_b = probs.astype(jnp.bfloat16)
    attended = jnp.einsum("chqk,ckhd->cqhd", probs_b, values_h, preferred_element_type=jnp.float32)
    attended = attended.astype(jnp.bfloat16).reshape(tok_rows, columns)
    out_terms = jnp.dot(attended, w_output, preferred_element_type=jnp.float32)
    layer_out = lax.psum_scatter(
        out_terms.astype(jnp.bfloat16), "tensor", scatter_dimension=1, tiled=True
    )
    grad_full = lax.all_gather(cotangent, "tensor", axis=1, tiled=True)
    grad_att = jnp.dot(grad_full, w_output.T, preferred_element_type=jnp.float32).astype(
        jnp.bfloat16
    )
    grad_output = jnp.dot(attended.T, grad_full, preferred_element_type=jnp.float32)
    grad_att_h = grad_att.reshape(span_count, SPAN, heads_here, HD)
    grad_prob = jnp.einsum(
        "cqhd,ckhd->chqk", grad_att_h, values_h, preferred_element_type=jnp.float32
    )
    inner = jnp.sum(grad_prob * probs, axis=-1, keepdims=True)
    grad_score = (probs * (grad_prob - inner) * scale).astype(jnp.bfloat16)
    grad_v = jnp.einsum("chqk,cqhd->ckhd", probs_b, grad_att_h, preferred_element_type=jnp.float32)
    grad_v = grad_v.astype(jnp.bfloat16).reshape(live_blocks * NB, columns)
    grad_q = jnp.einsum("chqk,ckhd->cqhd", grad_score, keys_h, preferred_element_type=jnp.float32)
    grad_q = grad_q.astype(jnp.bfloat16).reshape(tok_rows, columns)
    grad_k = jnp.einsum("chqk,cqhd->ckhd", grad_score, query_h, preferred_element_type=jnp.float32)
    grad_k = grad_k.astype(jnp.bfloat16).reshape(live_blocks * NB, columns)
    hidden_terms = jnp.dot(grad_q, w_query.T, preferred_element_type=jnp.float32)
    grad_hidden = lax.psum_scatter(
        hidden_terms.astype(jnp.bfloat16), "tensor", scatter_dimension=1, tiled=True
    )
    grad_query = jnp.dot(hidden_full.T, grad_q, preferred_element_type=jnp.float32)
    grad_key = jnp.dot(nbr_flat.T, grad_k, preferred_element_type=jnp.float32)
    grad_value = jnp.dot(nbr_flat.T, grad_v, preferred_element_type=jnp.float32)
    nbr_terms = jnp.dot(grad_k, w_key.T, preferred_element_type=jnp.float32)
    nbr_terms = nbr_terms + jnp.dot(grad_v, w_value.T, preferred_element_type=jnp.float32)
    share = lax.psum_scatter(
        nbr_terms.astype(jnp.bfloat16).reshape(live_blocks, NB, width),
        "tensor",
        scatter_dimension=1,
        tiled=True,
    )
    slot_grad = jnp.dot(
        select.T,
        share.reshape(live_blocks, block_part * width),
        preferred_element_type=jnp.float32,
    ).astype(jnp.bfloat16)
    returned = lax.all_to_all(
        slot_grad.reshape(n_shards, capacity, block_part, width),
        "dp",
        split_axis=0,
        concat_axis=0,
        tiled=True,
    )
    grad_encodings = jnp.dot(
        table.T,
        returned.reshape(slot_count, block_part * width),
        preferred_element_type=jnp.float32,
    )
    grad_encodings = grad_encodings.reshape(db_blocks, block_part, width)
    summed_q, summed_k, summed_v, summed_o = (
        lax.psum_scatter(
            grad_query.astype(jnp.bfloat16), "dp", scatter_dimension=0, tiled=True
        ).astype(jnp.float32),
        lax.psum_scatter(
            grad_key.astype(jnp.bfloat16), "dp", scatter_dimension=0, tiled=True
        ).astype(jnp.float32),
        lax.psum_scatter(
            grad_value.astype(jnp.bfloat16), "dp", scatter_dimension=0, tiled=True
        ).astype(jnp.float32),
        lax.psum_scatter(
            grad_output.astype(jnp.bfloat16), "dp", scatter_dimension=1, tiled=True
        ).astype(jnp.float32),
    )
    return (layer_out, grad_hidden, grad_encodings, summed_q, summed_k, summed_v, summed_o)


def solution(mesh):
    return jax.shard_map(
        shards,
        mesh=mesh,
        in_specs=(
            P("dp", "tensor"),
            P("dp", "tensor", None),
            P("dp", None),
            P("dp", None),
            P(None, "tensor"),
            P(None, "tensor"),
            P(None, "tensor"),
            P("tensor", None),
            P("dp", "tensor"),
        ),
        out_specs=(
            P("dp", "tensor"),
            P("dp", "tensor"),
            P("dp", "tensor", None),
            P("dp", "tensor"),
            P("dp", "tensor"),
            P("dp", "tensor"),
            P("tensor", "dp"),
        ),
        check_vma=False,
    )
```

```python
import math

import jax
import jax.numpy as jnp
from jax import lax
from jax.experimental import pallas as pl
from jax.experimental.pallas import tpu as pltpu
from jax.sharding import PartitionSpec as P

HD = 128
SPAN = 64
NB = 128
K_NBR = 2
BF16 = jnp.bfloat16
F32 = jnp.float32


def contract(a, b, dim_a, dim_b):
    return lax.dot_general(a, b, (((dim_a,), (dim_b,)), ((), ())), preferred_element_type=F32)


def softmax_of(q, k, scale):
    scores = contract(q, k, 1, 1) * scale
    top = jnp.max(scores, axis=-1, keepdims=True)
    e = jnp.exp(scores - top)
    return e / jnp.sum(e, axis=-1, keepdims=True)


def attend(query, keys, values, span_count, heads, scale):
    cols = heads * HD
    wide = K_NBR * NB

    def body(q_ref, k_ref, v_ref, o_ref):
        for h in range(heads):
            part = slice(h * HD, (h + 1) * HD)
            probs = softmax_of(q_ref[:, part], k_ref[:, part], scale).astype(BF16)
            o_ref[:, part] = contract(probs, v_ref[:, part], 1, 0).astype(BF16)

    tok = pl.BlockSpec((SPAN, cols), lambda c: (c, 0))
    nbr = pl.BlockSpec((wide, cols), lambda c: (c, 0))
    return pl.pallas_call(
        body,
        grid=(span_count,),
        in_specs=[tok, nbr, nbr],
        out_specs=tok,
        out_shape=jax.ShapeDtypeStruct((span_count * SPAN, cols), BF16),
        cost_estimate=pl.CostEstimate(
            flops=4 * span_count * SPAN * wide * cols,
            bytes_accessed=4 * span_count * (SPAN + wide) * cols,
            transcendentals=span_count * heads * SPAN * wide,
        ),
        name="attend",
    )(query, keys, values)


def attend_back(query, keys, values, grad_att, span_count, heads, scale):
    cols = heads * HD
    wide = K_NBR * NB

    def body(q_ref, k_ref, v_ref, g_ref, gq_ref, gk_ref, gv_ref):
        for h in range(heads):
            part = slice(h * HD, (h + 1) * HD)
            q, k, g = q_ref[:, part], k_ref[:, part], g_ref[:, part]
            probs = softmax_of(q, k, scale)
            grad_prob = contract(g, v_ref[:, part], 1, 1)
            inner = jnp.sum(grad_prob * probs, axis=-1, keepdims=True)
            grad_score = (probs * (grad_prob - inner) * scale).astype(BF16)
            gv_ref[:, part] = contract(probs.astype(BF16), g, 0, 0).astype(BF16)
            gq_ref[:, part] = contract(grad_score, k, 1, 0).astype(BF16)
            gk_ref[:, part] = contract(grad_score, q, 0, 0).astype(BF16)

    tok = pl.BlockSpec((SPAN, cols), lambda c: (c, 0))
    nbr = pl.BlockSpec((wide, cols), lambda c: (c, 0))
    toks = jax.ShapeDtypeStruct((span_count * SPAN, cols), BF16)
    nbrs = jax.ShapeDtypeStruct((span_count * wide, cols), BF16)
    return pl.pallas_call(
        body,
        grid=(span_count,),
        in_specs=[tok, nbr, nbr, tok],
        out_specs=[tok, nbr, nbr],
        out_shape=[toks, nbrs, nbrs],
        cost_estimate=pl.CostEstimate(
            flops=12 * span_count * SPAN * wide * cols,
            bytes_accessed=4 * span_count * (2 * SPAN + 2 * wide) * cols,
            transcendentals=span_count * heads * SPAN * wide,
        ),
        name="attend_back",
    )(query, keys, values, grad_att)


def block_products(me, left, right, count, odd, cut_left):
    depth = left.shape[0]
    rows, cols = left.shape[1], right.shape[1]
    if cut_left:
        rows //= count
        left_spec = pl.BlockSpec((depth, rows), lambda i, m: (0, m[0] ^ (2 * i + odd)))
        right_spec = pl.BlockSpec((depth, cols), lambda i, m: (0, 0))
    else:
        cols //= count
        left_spec = pl.BlockSpec((depth, rows), lambda i, m: (0, 0))
        right_spec = pl.BlockSpec((depth, cols), lambda i, m: (0, m[0] ^ (2 * i + odd)))

    def body(m_ref, l_ref, r_ref, o_ref):
        o_ref[0] = contract(l_ref[...], r_ref[...], 0, 0).astype(BF16)

    half = count // 2
    return pl.pallas_call(
        body,
        grid_spec=pltpu.PrefetchScalarGridSpec(
            num_scalar_prefetch=1,
            grid=(half,),
            in_specs=[left_spec, right_spec],
            out_specs=pl.BlockSpec((1, rows, cols), lambda i, m: (i, 0, 0)),
        ),
        out_shape=jax.ShapeDtypeStruct((half, rows, cols), BF16),
        cost_estimate=pl.CostEstimate(
            flops=2 * half * depth * rows * cols,
            bytes_accessed=2 * (depth * (rows + cols) * half + half * rows * cols),
            transcendentals=0,
        ),
        name="block_products",
    )(me, left, right)


def block_pairs(me, first, second, odd):
    count, rows, cols = first.shape
    half = count // 2

    def body(m_ref, a_ref, b_ref, o_ref):
        o_ref[0, 0] = a_ref[0]
        o_ref[0, 1] = b_ref[0]

    spec = pl.BlockSpec((1, rows, cols), lambda i, m: (m[0] ^ (2 * i + odd), 0, 0))
    return pl.pallas_call(
        body,
        grid_spec=pltpu.PrefetchScalarGridSpec(
            num_scalar_prefetch=1,
            grid=(half,),
            in_specs=[spec, spec],
            out_specs=pl.BlockSpec((1, 2, rows, cols), lambda i, m: (i, 0, 0, 0)),
        ),
        out_shape=jax.ShapeDtypeStruct((half, 2, rows, cols), BF16),
        cost_estimate=pl.CostEstimate(
            flops=0, bytes_accessed=8 * half * rows * cols, transcendentals=0
        ),
        name="block_pairs",
    )(me, first, second)


def halving(send, keep, count, axis):
    bits = count.bit_length() - 1

    def pairs(bit):
        return [(i, i ^ (1 << bit)) for i in range(count)]

    got = lax.ppermute(send, axis, pairs(0))
    middle = keep.shape[1] // 2
    tail = (middle,) + keep.shape[2:]
    ended = []
    for half in range(2):
        mine = keep[:, half * middle : (half + 1) * middle].reshape((2,) * (bits - 1) + tail)
        other = got[:, half * middle : (half + 1) * middle].reshape(mine.shape)
        order = list(range(bits - 1, 0, -1)) if half else list(range(1, bits))
        dims = list(range(bits - 1, 0, -1))
        for bit in order:
            dim = dims.index(bit)
            outgoing = lax.index_in_dim(mine, 1, dim, False) + lax.index_in_dim(
                other, 1, dim, False
            )
            mine = lax.index_in_dim(mine, 0, dim, False) + lax.index_in_dim(other, 0, dim, False)
            other = lax.ppermute(outgoing, axis, pairs(bit))
            dims.remove(bit)
        ended.append(mine.astype(F32) + other.astype(F32))
    return ended


def shards(hidden_in, encodings, nbr_shard, nbr_row, w_query, w_key, w_value, w_output, cotangent):
    n_shards = lax.axis_size("dp")
    tok_rows = hidden_in.shape[0]
    columns = w_query.shape[1]
    heads_here = columns // HD
    span_count = tok_rows // SPAN
    live_blocks = K_NBR * span_count
    capacity = max(2, 4 * span_count // n_shards)
    slot_count = n_shards * capacity
    db_blocks = encodings.shape[0]
    block_part = encodings.shape[1]
    width = encodings.shape[2]
    scale = 1.0 / math.sqrt(HD)
    me = lax.axis_index("dp").astype(jnp.int32).reshape(1)

    hidden_full = lax.all_gather(hidden_in, "tensor", axis=1, tiled=True)

    owners = nbr_shard.reshape(live_blocks)
    rowids = nbr_row.reshape(live_blocks)
    order = jnp.arange(live_blocks, dtype=jnp.int32)
    earlier = (owners[:, None] == owners[None, :]) & (order[None, :] < order[:, None])
    position = jnp.sum(earlier.astype(jnp.int32), axis=1)
    slot_of = owners * capacity + position
    picked = slot_of[:, None] == jnp.arange(slot_count, dtype=jnp.int32)[None, :]
    request = jnp.sum(jnp.where(picked, rowids[:, None] + 1, 0), axis=0) - 1
    wanted = lax.all_to_all(
        request.reshape(n_shards, capacity), "dp", split_axis=0, concat_axis=0, tiled=True
    )
    table = (
        wanted.reshape(slot_count)[:, None] == jnp.arange(db_blocks, dtype=jnp.int32)[None, :]
    ).astype(BF16)
    outgoing = contract(table, encodings.reshape(db_blocks, block_part * width), 1, 0)
    outgoing = outgoing.astype(BF16).reshape(n_shards, capacity, block_part, width)
    arrived = lax.all_to_all(outgoing, "dp", split_axis=0, concat_axis=0, tiled=True)
    select = picked.astype(BF16)
    live = contract(select, arrived.reshape(slot_count, block_part * width), 1, 0)
    live = live.astype(BF16).reshape(live_blocks, block_part, width)
    neighbours = lax.all_gather(live, "tensor", axis=1, tiled=True)
    nbr_flat = neighbours.reshape(live_blocks * NB, width)

    query = contract(hidden_full, w_query, 1, 0).astype(BF16)
    keys = contract(nbr_flat, w_key, 1, 0).astype(BF16)
    values = contract(nbr_flat, w_value, 1, 0).astype(BF16)
    cotangent, keys = lax.optimization_barrier((cotangent, keys))
    grad_full = lax.all_gather(cotangent, "tensor", axis=1, tiled=True)

    attended = attend(query, keys, values, span_count, heads_here, scale)
    out_terms = contract(attended, w_output, 1, 0).astype(BF16)
    layer_out = lax.psum_scatter(out_terms, "tensor", scatter_dimension=1, tiled=True)

    grad_att = contract(grad_full, w_output, 1, 1).astype(BF16)
    grad_q, grad_k, grad_v = attend_back(
        query, keys, values, grad_att, span_count, heads_here, scale
    )
    nbr_terms = contract(grad_k, w_key, 1, 1) + contract(grad_v, w_value, 1, 1)
    nbr_terms = nbr_terms.astype(BF16).reshape(live_blocks, NB, width)
    nbr_terms, grad_q = lax.optimization_barrier((nbr_terms, grad_q))
    share = lax.psum_scatter(nbr_terms, "tensor", scatter_dimension=1, tiled=True)
    hidden_terms = contract(grad_q, w_query, 1, 1).astype(BF16)
    grad_hidden = lax.psum_scatter(hidden_terms, "tensor", scatter_dimension=1, tiled=True)

    sent_o = block_products(me, attended, grad_full, n_shards, 1, False)
    kept_o = block_products(me, attended, grad_full, n_shards, 0, False)
    summed_o = jnp.concatenate(halving(sent_o, kept_o, n_shards, "dp"), axis=0)
    sent_q = block_products(me, hidden_full, grad_q, n_shards, 1, True)
    kept_q = block_products(me, hidden_full, grad_q, n_shards, 0, True)
    summed_q = jnp.concatenate(halving(sent_q, kept_q, n_shards, "dp"), axis=0)
    stack = (n_shards, width // n_shards, columns)
    grad_key = contract(nbr_flat, grad_k, 0, 0).astype(BF16).reshape(stack)
    grad_value = contract(nbr_flat, grad_v, 0, 0).astype(BF16).reshape(stack)
    sent_kv = block_pairs(me, grad_key, grad_value, 1)
    kept_kv = block_pairs(me, grad_key, grad_value, 0)
    summed_k, summed_v = halving(sent_kv, kept_kv, n_shards, "dp")

    slot_grad = contract(select, share.reshape(live_blocks, block_part * width), 0, 0).astype(BF16)
    returned = lax.all_to_all(
        slot_grad.reshape(n_shards, capacity, block_part, width),
        "dp",
        split_axis=0,
        concat_axis=0,
        tiled=True,
    )
    grad_encodings = contract(table, returned.reshape(slot_count, block_part * width), 0, 0)
    grad_encodings = grad_encodings.reshape(db_blocks, block_part, width)
    return (
        layer_out,
        grad_hidden,
        grad_encodings,
        summed_q,
        summed_k.reshape(width // n_shards, columns),
        summed_v.reshape(width // n_shards, columns),
        summed_o,
    )


def solution(mesh):
    return jax.shard_map(
        shards,
        mesh=mesh,
        in_specs=(
            P("dp", "tensor"),
            P("dp", "tensor", None),
            P("dp", None),
            P("dp", None),
            P(None, "tensor"),
            P(None, "tensor"),
            P(None, "tensor"),
            P("tensor", None),
            P("dp", "tensor"),
        ),
        out_specs=(
            P("dp", "tensor"),
            P("dp", "tensor"),
            P("dp", "tensor", None),
            P("dp", "tensor"),
            P("dp", "tensor"),
            P("dp", "tensor"),
            P("tensor", "dp"),
        ),
        check_vma=False,
    )
```
